256 devices in a mesh: member: 8 (over y, x_lo), pix: 32 (over x_hi, z, core).
Axes of the slice: x: 4 (x_hi: 2, x_lo: 2; x = x_hi * 2 + x_lo), y: 4, z: 8, core: 2. Of those that a mesh axis runs over, the one named last changes fastest.
Arguments:
- field: bfloat16 [16, 256, 512, 128], P('member', 'pix'), may hold values from -17 to 17
- dw_kernel: float32 [2, 7, 7, 128], replicated, may hold values from -0.875 to 0.875
- dw_bias: float32 [2, 128], replicated, may hold values from -3 to 3
- ln_gain: float32 [2, 128], replicated, may hold values from 0.25 to 1.75
- w_in: bfloat16 [2, 128, 512], replicated, may hold values from -0.5 to 0.5
- b_in: float32 [2, 512], replicated, may hold values from -3 to 3
- w_out: bfloat16 [2, 512, 128], replicated, may hold values from -0.25 to 0.25
- attn_gain: float32 [128], replicated, may hold values from 0.25 to 1.75
- w_qkv: bfloat16 [128, 384], replicated, may hold values from -11 to 11
- w_proj: bfloat16 [128, 128], replicated, may hold values from -0.5 to 0.5
Outputs:
- refined: bfloat16 [16, 256, 512, 128], P('member', 'pix')
- attended: bfloat16 [16, 32, 64, 128], P('member', 'pix')
The draws below stay inside these ranges and needn't reach their ends.
All inputs are finite; a program needn't handle non-finite values.
Results may differ from the reference program's by a relative error of at most 0.012.
Values may be sent and summed in bfloat16 or wider, within the bound.
No kernel may reach another device: no remote copies, remote signals or barrier semaphores. Data moves between devices by JAX's collectives and lax.ppermute only.
A program may use at most 64 MiB of HBM per device.

```python
import math
import jax
import jax.numpy as jnp
from jax import lax

C = 128
HID = 512
HEADS = 4
KS = 7
LAYERS = 2
POOL = 8
COLS = 512
HEAD_DIM = 32
MEMBERS = 16
ROWS = 256
CROWS = 32
CCOLS = 64


def draw_field(key, part):
    key_member = jax.random.fold_in(key, 12)
    key_scale = jax.random.fold_in(key, 13)
    member_part = jax.random.truncated_normal(key_member, -4.0, 4.0, (MEMBERS, ROWS, COLS, C), jnp.float32)
    channel_scale = jnp.exp(jax.random.uniform(key_scale, (C,), jnp.float32, math.log(0.3), math.log(3.0)))
    values = member_part
    return (values * channel_scale).astype(jnp.bfloat16)


def draw_w_qkv(key, part):
    key_entries = jax.random.fold_in(key, 21)
    entries = jax.random.truncated_normal(key_entries, -3.0, 3.0, (C, 3 * C), jnp.float32) * C ** (-0.5)
    entries = jnp.concatenate([entries[:, :C] * 4.0, entries[:, C:]], axis=1)
    return entries.astype(jnp.bfloat16)


def scatter_about(stream_key, dims, scale, most, kind=jnp.bfloat16):
    drawn = scale * jax.random.normal(stream_key, dims, jnp.float32)
    return jnp.clip(drawn, min=-most, max=most).astype(kind)


def setup_inputs(seed: int = 0) -> dict:
    key_of = jax.random.split(jax.random.key(seed), 11)
    field = draw_field(jax.random.fold_in(key_of[10], 71), 0)
    dw_kernel = scatter_about(key_of[1], (LAYERS, KS, KS, C), 0.15, 0.875, jnp.float32)
    dw_bias = scatter_about(key_of[2], (LAYERS, C), 0.5, 3.0, jnp.float32)
    ln_gain = jnp.clip(1.0 + 0.15 * jax.random.normal(key_of[3], (LAYERS, C), jnp.float32), 0.25, 1.75)
    w_in = scatter_about(key_of[4], (LAYERS, C, HID), C ** -0.5, 0.5)
    b_in = scatter_about(key_of[5], (LAYERS, HID), 0.5, 3.0, jnp.float32)
    w_out = scatter_about(key_of[6], (LAYERS, HID, C), HID ** -0.5, 0.25)
    attn_gain = jnp.clip(1.0 + 0.15 * jax.random.normal(key_of[7], (C,), jnp.float32), 0.25, 1.75)
    w_qkv = draw_w_qkv(jax.random.fold_in(key_of[10], 71), 0)
    w_proj = scatter_about(key_of[9], (C, C), C ** -0.5, 0.5)
    return dict(field=field, dw_kernel=dw_kernel, dw_bias=dw_bias, ln_gain=ln_gain, w_in=w_in, b_in=b_in, w_out=w_out, attn_gain=attn_gain, w_qkv=w_qkv, w_proj=w_proj)


def layer_norm(values, scaling):
    centre = lax.optimization_barrier(jnp.mean(values, -1, keepdims=True))
    centred = values - centre
    spread = lax.optimization_barrier(jnp.mean(centred * centred, -1, keepdims=True))
    return centred * lax.rsqrt(spread + 1e-06) * scaling

def depthwise(extended, kernel, offset):
    kernel_side = kernel.shape[0]
    margin = kernel_side // 2
    out_rows = extended.shape[1] - 2 * margin
    columns = extended.shape[2]
    padded = jnp.pad(extended, ((0, 0), (0, 0), (margin, margin), (0, 0)))
    summed = jnp.zeros((extended.shape[0], out_rows, columns, extended.shape[3]), jnp.float32) + offset
    for row_off in range(kernel_side):
        for col_off in range(kernel_side):
            window = padded[:, row_off:row_off + out_rows, col_off:col_off + columns].astype(jnp.float32)
            summed = summed + window * kernel[row_off, col_off]
    return summed

def convnext(extended, kernel, offset, scaling, w_first, b_first, w_second):
    margin = kernel.shape[0] // 2
    filtered = depthwise(extended, kernel, offset)
    out_shape = filtered.shape
    channels = out_shape[3]
    normed = layer_norm(filtered, scaling).astype(jnp.bfloat16).reshape(-1, channels)
    before = jnp.dot(normed, w_first, preferred_element_type=jnp.float32) + b_first
    hidden = jax.nn.gelu(before, approximate=True).astype(jnp.bfloat16)
    branch = jnp.dot(hidden, w_second, preferred_element_type=jnp.float32).reshape(out_shape)
    centre_rows = extended[:, margin:margin + out_shape[1]].astype(jnp.float32)
    return (centre_rows + branch).astype(jnp.bfloat16)

def reference(field, dw_kernel, dw_bias, ln_gain, w_in, b_in, w_out, attn_gain, w_qkv, w_proj):
    margin = KS // 2

    def refine(member_field):
        current = member_field[None]
        for layer_index in range(LAYERS):
            extended = jnp.pad(current, ((0, 0), (margin, margin), (0, 0), (0, 0)))
            current = convnext(extended, dw_kernel[layer_index], dw_bias[layer_index], ln_gain[layer_index], w_in[layer_index], b_in[layer_index], w_out[layer_index])
        refined_member = current[0]
        pooled_member = refined_member.astype(jnp.float32).reshape(CROWS, POOL, CCOLS, POOL, C).mean(axis=(1, 3))
        return (refined_member, pooled_member)
    refined, pooled = lax.map(refine, field)
    cells = CROWS * CCOLS
    pooled_normed = layer_norm(pooled, attn_gain).astype(jnp.bfloat16).reshape(MEMBERS * cells, C)
    projected = jnp.dot(pooled_normed, w_qkv, preferred_element_type=jnp.float32).astype(jnp.bfloat16)
    projected = projected.reshape(MEMBERS, cells, 3, HEADS, HEAD_DIM)
    queries = projected[:, :, 0].astype(jnp.float32)
    keys_all = projected[:, :, 1].astype(jnp.float32)
    values_all = projected[:, :, 2].astype(jnp.float32)
    scores = jnp.einsum('mphd,nphd->mpnh', queries, keys_all) / math.sqrt(HEAD_DIM)
    weights = jax.nn.softmax(scores, axis=2).astype(jnp.bfloat16)
    blended = jnp.einsum('mpnh,nphd->mphd', weights.astype(jnp.float32), values_all)
    blended = blended.astype(jnp.bfloat16).reshape(MEMBERS * cells, C)
    mixed = jnp.dot(blended, w_proj, preferred_element_type=jnp.float32)
    attended = (pooled.reshape(MEMBERS * cells, C) + mixed).astype(jnp.bfloat16).reshape(MEMBERS, CROWS, CCOLS, C)
    return (refined, attended)
```

```python
import functools

import jax
import jax.numpy as jnp
from jax import lax
from jax.experimental import pallas as pl
from jax.experimental.pallas import tpu as pltpu
from jax.sharding import PartitionSpec as P

bf16, f32 = jnp.bfloat16, jnp.float32
HEADS = 4
POOL = 8
KS = 7
PAD = KS // 2
C = 128
JB = 8


def fill_edges(xs, row, run):
    sub = lax.broadcasted_iota(jnp.int32, (8, C), 0)
    for q in range(PAD):
        v = xs[row, run + q].astype(f32)
        a, b = pltpu.roll(v[:, :C], 1, 0), pltpu.roll(v[:, C:], 1, 0)
        v = jnp.concatenate([jnp.where(sub == 0, 0.0, a), jnp.where(sub == 0, a, b)], 1)
        xs[row, q] = v.astype(bf16)
        v = xs[row, PAD + q].astype(f32)
        a, b = pltpu.roll(v[:, :C], 7, 0), pltpu.roll(v[:, C:], 7, 0)
        v = jnp.concatenate([jnp.where(sub == 7, b, a), jnp.where(sub == 7, 0.0, b)], 1)
        xs[row, PAD + run + q] = v.astype(bf16)


def block_kernel(first, layer, rows, run, n_in, *refs):
    x_ref, top_ref, bot_ref, dwk_ref, dwb_ref, gain_ref, w1_ref, b1_ref, w2_ref = refs[:9]
    if first:
        y_ref, ytop_ref, ybot_ref, xs, kb, w2s, xf = refs[n_in:]
    else:
        attn_ref = refs[9]
        y_ref, pool_ref, normed_ref, xs, kb, w2s, xf, acc = refs[n_in:]
    r = pl.program_id(1)

    @pl.when(r == 0)
    def _():
        for t in range(KS * KS):
            k = jnp.broadcast_to(dwk_ref[0, t // KS, pl.ds(t % KS, 1), :], (8, C))
            kb[t] = jnp.concatenate([k, k], 1).astype(bf16)
        w2s[...] = w2_ref[0] * bf16(0.5)

        def put(src, i, row):
            if first:
                xf[...] = src[0, i].astype(f32)
                for j in range(run):
                    a = xf[pl.ds(j, 8, stride=run), :]
                    b = xf[pl.ds(8 * run + j, 8, stride=run), :]
                    xs[row, PAD + j] = jnp.concatenate([a, b], 1).astype(bf16)
            else:
                xs[row, PAD:PAD + run] = src[0, i]
            fill_edges(xs, row, run)

        def edge(i, _):
            put(top_ref, i, i)
            put(bot_ref, i, i + PAD + rows)
            return 0

        def own(i, _):
            put(x_ref, i, i + PAD)
            return 0

        lax.fori_loop(0, PAD, edge, 0)
        lax.fori_loop(0, rows, own, 0)
        if not first:
            acc[...] = jnp.zeros_like(acc)

    bias = dwb_ref[layer:layer + 1, :]
    gain = gain_ref[layer:layer + 1, :]
    b1 = b1_ref[layer:layer + 1, :]
    for jb in range(run // JB):
        tot = [None] * JB
        for dr in range(KS):
            ks = [kb[dr * KS + dw] for dw in range(KS)]
            xv = [xs[r + dr, jb * JB + q] for q in range(JB + KS - 1)]
            for o in range(JB):
                p = [xv[o + dw] * ks[dw] for dw in range(KS)]
                part = ((p[0] + p[1]) + (p[2] + p[3])) + ((p[4] + p[5]) + p[6])
                tot[o] = part if tot[o] is None else tot[o] + part
        tf = [t.astype(f32) for t in tot]
        f = jnp.concatenate([t[:, :C] for t in tf] + [t[:, C:] for t in tf], 0) + bias
        cen = f - jnp.mean(f, -1, keepdims=True)
        var = jnp.mean(cen * cen, -1, keepdims=True)
        normed = (cen * lax.rsqrt(var + 1e-6) * gain).astype(bf16)
        u = (jnp.dot(normed, w1_ref[0], preferred_element_type=f32) + b1).astype(bf16)
        t = u * (u * u * bf16(0.7978845608 * 0.044715) + bf16(0.7978845608))
        br = jnp.dot(u * jnp.tanh(t) + u, w2s[...], preferred_element_type=f32)
        p = None
        for j in range(JB):
            xc = xs[r + PAD, PAD + jb * JB + j].astype(f32)
            y = xc + jnp.concatenate([br[j * 8:j * 8 + 8], br[(JB + j) * 8:(JB + j) * 8 + 8]], 1)
            y = y.astype(bf16)
            if first:
                y_ref[0, 0, jb * JB + j] = y
            else:
                v = y.astype(f32)
                p = v if p is None else p + v
                xf[pl.ds(jb * JB + j, 8, stride=run), :] = v[:, :C]
                xf[pl.ds(8 * run + jb * JB + j, 8, stride=run), :] = v[:, C:]
        if not first:
            acc[jb] += p
    if first:
        @pl.when(r < PAD)
        def _():
            ytop_ref[0, r] = y_ref[0, 0]

        @pl.when(r >= rows - PAD)
        def _():
            ybot_ref[0, r - (rows - PAD)] = y_ref[0, 0]
    else:
        y_ref[0, 0] = xf[...].astype(bf16)

        @pl.when(r == rows - 1)
        def _():
            v = acc[...].reshape(run // JB * 8, 2 * C) * (1.0 / (POOL * POOL))
            v = jnp.concatenate([v[:, :C], v[:, C:]], 0)
            pool_ref[0] = v
            cen = v - jnp.mean(v, -1, keepdims=True)
            var = jnp.mean(cen * cen, -1, keepdims=True)
            normed_ref[0] = (cen * lax.rsqrt(var + 1e-6) * attn_ref[...]).astype(bf16)


def convnext(first, layer, member, members, x, top, bot, weights, out=None):
    rows = x.shape[1]
    columns = x.shape[2] if first else x.shape[2] * 16
    run = columns // 16
    cells = columns // POOL
    side = (run, 8, 2 * C)
    dwk, dwb, gain, w1, b1, w2, attn_gain = weights

    def part(a, at=0):
        return pl.BlockSpec((1,) + a.shape[1:], lambda m, r: (at,) + (0,) * (a.ndim - 1))

    def whole(a):
        return pl.BlockSpec(a.shape, lambda m, r: (0,) * a.ndim)

    args = [x, top, bot, dwk, dwb, gain, w1, b1, w2]
    specs = [part(x, member if first else 0), part(top), part(bot), part(dwk, layer), whole(dwb), whole(gain),
             part(w1, layer), whole(b1), part(w2, layer)]
    scratch = [
        pltpu.VMEM((rows + 2 * PAD, run + 2 * PAD, 8, 2 * C), bf16),
        pltpu.VMEM((KS * KS, 8, 2 * C), bf16),
        pltpu.VMEM(w2.shape[1:], bf16),
        pltpu.VMEM((columns, C), f32),
    ]
    alias = {}
    if first:
        shapes = [jax.ShapeDtypeStruct((1, rows) + side, bf16)] + [jax.ShapeDtypeStruct((1, PAD) + side, bf16)] * 2
        outs = [pl.BlockSpec((1, 1) + side, lambda m, r: (0, r, 0, 0, 0))]
        outs += [pl.BlockSpec((1, PAD) + side, lambda m, r: (0, 0, 0, 0, 0))] * 2
    else:
        args.append(attn_gain)
        specs.append(whole(attn_gain))
        if out is not None:
            alias = {len(args): 0}
            args.append(out)
            specs.append(pl.BlockSpec(memory_space=pl.ANY))
        shapes = [
            jax.ShapeDtypeStruct((members, rows, columns, C), bf16),
            jax.ShapeDtypeStruct((1, cells, C), f32),
            jax.ShapeDtypeStruct((1, cells, C), bf16),
        ]
        outs = [pl.BlockSpec((1, 1, columns, C), lambda m, r: (member, r, 0, 0))]
        outs += [pl.BlockSpec((1, cells, C), lambda m, r: (0, 0, 0))] * 2
        scratch.append(pltpu.VMEM((run // JB, 8, 2 * C), f32))
    positions = rows * columns
    return pl.pallas_call(
        functools.partial(block_kernel, first, layer, rows, run, len(args)),
        out_shape=shapes,
        grid=(1, rows),
        in_specs=specs,
        out_specs=outs,
        scratch_shapes=scratch,
        input_output_aliases=alias,
        name="convnext_first" if first else "convnext_last",
        compiler_params=pltpu.CompilerParams(vmem_limit_bytes=40 << 20),
        cost_estimate=pl.CostEstimate(
            flops=positions * C * (4 * 512 + 98), bytes_accessed=4 * positions * C, transcendentals=positions * 512
        ),
    )(*args)


def attention_kernel(members, total, cells, feats_ref, own_ref, pool_ref, wqkv_ref, wproj_ref, out_ref, order):
    wqkv = wqkv_ref[...]
    own = jnp.concatenate([own_ref[m] for m in range(members)], 0)
    q = jnp.dot(own, wqkv[:, :C], preferred_element_type=f32).astype(bf16).astype(f32)
    feats = feats_ref[...].reshape(total * cells, C)
    kv = jnp.dot(feats, wqkv[:, C:], preferred_element_type=f32).astype(bf16).astype(f32)
    head = C // HEADS
    row_head = lax.broadcasted_iota(jnp.int32, (2 * C, C), 0) % C // head
    col_head = lax.broadcasted_iota(jnp.int32, (2 * C, C), 1) // head
    ones = jnp.where(row_head == col_head, 1.0, 0.0).astype(bf16)
    blended = []
    for m in range(members):
        qm = q[m * cells:(m + 1) * cells]
        scores = []
        for n in range(total):
            prod = qm * kv[n * cells:(n + 1) * cells, :C]
            high = prod.astype(bf16)
            low = (prod - high.astype(f32)).astype(bf16)
            both = jnp.concatenate([high, low], 1)
            scores.append(jnp.dot(both, ones, preferred_element_type=f32) * (1.0 / head ** 0.5))
        most = functools.reduce(jnp.maximum, scores)
        exps = [jnp.exp(s - most) for s in scores]
        inverse = 1.0 / functools.reduce(jnp.add, exps)
        mix = None
        for n in range(total):
            w = (exps[n] * inverse).astype(bf16).astype(f32)
            term = w * kv[n * cells:(n + 1) * cells, C:]
            mix = term if mix is None else mix + term
        blended.append(mix.astype(bf16))
    mixed = jnp.dot(jnp.concatenate(blended, 0), wproj_ref[...], preferred_element_type=f32)
    across = cells // 16
    for m in range(members):
        v = pool_ref[m] + mixed[m * cells:(m + 1) * cells]
        for i in range(2 * across):
            half, jj = i // across, i % across
            order[pl.ds(half * 8 * across + jj, 8, stride=across), :] = v[i * 8:(i + 1) * 8]
        out_ref[m, 0] = order[...].astype(bf16)


def attend(feats, own, pooled, wqkv, wproj):
    members, cells, _ = own.shape
    vmem = pl.BlockSpec(memory_space=pltpu.VMEM)
    return pl.pallas_call(
        functools.partial(attention_kernel, members, feats.shape[0], cells),
        out_shape=jax.ShapeDtypeStruct((members, 1, cells, C), bf16),
        in_specs=[vmem] * 5,
        out_specs=vmem,
        scratch_shapes=[pltpu.VMEM((cells, C), f32)],
        name="member_attention",
    )(feats, own, pooled, wqkv, wproj)


def gather_members(value):
    copies = jnp.broadcast_to(value, (lax.axis_size("member"), *value.shape))
    return lax.all_to_all(copies, "member", split_axis=0, concat_axis=0, tiled=True)


def on_device(field, dw_kernel, dw_bias, ln_gain, w_in, b_in, w_out, attn_gain, w_qkv, w_proj):
    members, rows, columns, channels = field.shape
    size = lax.axis_size("pix")
    up = [(i, i + 1) for i in range(size - 1)]
    down = [(j, i) for i, j in up]
    weights = (dw_kernel, dw_bias, ln_gain, w_in, b_in, w_out, attn_gain.reshape(1, channels))
    halos = []
    for m in range(members):
        halos.append((
            lax.ppermute(field[m:m + 1, rows - PAD:], "pix", up),
            lax.ppermute(field[m:m + 1, :PAD], "pix", down),
        ))
    middle = []
    for m in range(members):
        y, ytop, ybot = convnext(True, 0, m, members, field, *halos[m], weights)
        middle.append((y, lax.ppermute(ybot, "pix", up), lax.ppermute(ytop, "pix", down)))
    refined, pooled, normed = None, [], []
    for m in range(members):
        refined, p, z = convnext(False, 1, m, members, *middle[m], weights, out=refined)
        pooled.append(p)
        normed.append(z)
    pooled = jnp.concatenate(pooled, 0)
    normed = jnp.concatenate(normed, 0)
    cells = normed.shape[1]
    feats = gather_members(normed).reshape(-1, cells, channels)
    attended = attend(feats, normed, pooled, w_qkv, w_proj)
    return refined, attended


def solution(mesh):
    placed = (P("member", "pix", None, None), P(), P(), P(), P(), P(), P(), P(), P(), P())
    return jax.shard_map(
        on_device,
        mesh=mesh,
        in_specs=placed,
        out_specs=(P("member", "pix", None, None), P("member", "pix", None, None)),
        check_vma=False,
    )
```
